128 devices in a mesh: cls: 4 (over y_lo, core), grp: 32 (over x, y_hi, z).
Axes of the slice: x: 4, y: 4 (y_hi: 2, y_lo: 2; y = y_hi * 2 + y_lo), z: 4, core: 2. Of those that a mesh axis runs over, the one named last changes fastest.
Arguments:
- images: bfloat16 [1024, 9216], P(('cls', 'grp')), may hold values from -40 to 40
- ctf: bfloat16 [1024, 64], P(('cls', 'grp')), may hold values from -1 to 1
- refs: bfloat16 [512, 9216], P('cls'), may hold values from -12 to 12
- noise_inv: float32 [64], replicated, may hold values from 0.006 to 0.024
- reg: float32 [64], replicated, may hold values from 0.01 to 0.1
Outputs:
- new_refs: float32 [512, 9216], P('cls')
The draws below stay inside these ranges and needn't reach their ends.
All inputs are finite; a program needn't handle non-finite values.
Results may differ from the reference program's by a relative error of at most 0.004.
Values may be sent and summed in bfloat16 or wider, within the bound.
A program may use at most 192 MiB of HBM per device.

```python
import math
import jax
import jax.numpy as jnp
from jax import lax

CLASSES = 512
CYCLES = 64
ANGLES = 72
ROT = 36
PIX = 9216
NPART = 1024


mean_precision = 0.013


noise_level = 3.0


def shared_draws(key):
    spread = math.sqrt(3.0 * (math.log(ROT * CLASSES) + 0.5) / (PIX * mean_precision))
    class_table = spread * jax.random.truncated_normal(jax.random.fold_in(key, 11), -4.0, 4.0, (CLASSES, PIX), jnp.float32)
    contrast = jax.random.uniform(jax.random.fold_in(key, 12), (NPART, CYCLES), jnp.float32, -1.0, 1.0)
    owner = jax.random.permutation(jax.random.fold_in(key, 13), NPART) % CLASSES
    turns = jax.random.randint(jax.random.fold_in(key, 14), (NPART,), 0, ROT)
    return (class_table, contrast, owner.astype(jnp.int32), turns.astype(jnp.int32))


def draw_refs(key, part):
    class_table, contrast, owner, turns = shared_draws(key)
    return class_table.astype(jnp.bfloat16)


def draw_ctf(key, part):
    class_table, contrast, owner, turns = shared_draws(key)
    return contrast.astype(jnp.bfloat16)


def draw_images(key, part):
    class_table, contrast, owner, turns = shared_draws(key)
    step = ANGLES // ROT * 2 * CYCLES
    chosen = class_table[owner]
    column = jnp.arange(PIX, dtype=jnp.int32)
    source = (column[None, :] - (turns * step)[:, None]) % PIX
    turned = jnp.take_along_axis(chosen, source, axis=1)
    signal = turned * jnp.tile(contrast, (1, 2 * ANGLES))
    shape = (NPART, PIX)
    level = noise_level * jnp.exp(jax.random.uniform(jax.random.fold_in(key, 21), (NPART,), jnp.float32, math.log(0.7), math.log(1.4)))
    noise = jax.random.truncated_normal(jax.random.fold_in(key, 22), -4.0, 4.0, shape, jnp.float32)
    result = signal + level[:, None] * noise
    return result.astype(jnp.bfloat16)


def setup_inputs(seed: int = 0) -> dict:
    keys = jax.random.split(jax.random.key(seed), 6)
    images = draw_images(jax.random.fold_in(keys[5], 71), 0)
    ctf = draw_ctf(jax.random.fold_in(keys[5], 71), 0)
    refs = draw_refs(jax.random.fold_in(keys[5], 71), 0)
    noise_inv = jnp.clip(jnp.exp(jax.random.uniform(keys[3], (CYCLES,), jnp.float32, math.log(0.006), math.log(0.024))), 0.006, 0.024)
    reg = jnp.clip(jnp.exp(jax.random.uniform(keys[4], (CYCLES,), jnp.float32, math.log(0.01), math.log(0.1))), 0.01, 0.1)
    return {"images": images, "ctf": ctf, "refs": refs, "noise_inv": noise_inv, "reg": reg}


def cycle_table():
    column = jnp.arange(PIX, dtype=jnp.int32) % CYCLES
    return (column[:, None] == jnp.arange(CYCLES, dtype=jnp.int32)[None, :]).astype(jnp.float32)


def prepare(images, ctf, noise_inv):
    ctf_value = ctf.astype(jnp.float32)
    factor = ctf_value * noise_inv[None, :]
    values = images.astype(jnp.float32)
    weighted = (values * jnp.tile(factor, (1, 2 * ANGLES))).astype(jnp.bfloat16)
    noise_row = jnp.tile(noise_inv, 2 * ANGLES)
    offset = 0.5 * jnp.sum(values * values * noise_row[None, :], axis=1)
    curve = factor * ctf_value
    return weighted, offset, curve


def rolled_range(weighted, first, count):
    rows = weighted.shape[0]
    step = (ANGLES // ROT) * 2 * CYCLES
    turned = [jnp.roll(weighted, -(first + rotation) * step, axis=1) for rotation in range(count)]
    return jnp.stack(turned, axis=1).reshape(rows * count, PIX)


def class_power(refs):
    values = refs.astype(jnp.float32)
    return jnp.dot(values * values, cycle_table(), precision=lax.Precision.HIGHEST)


def reference(images, ctf, refs, noise_inv, reg):
    power = class_power(refs)
    block = math.gcd(NPART, 256)
    starts = jnp.arange(NPART // block, dtype=jnp.int32) * block

    def one_block(carry, start):
        numer, denom = carry
        part_images = lax.dynamic_slice_in_dim(images, start, block, 0)
        part_ctf = lax.dynamic_slice_in_dim(ctf, start, block, 0)
        weighted, offset, curve = prepare(part_images, part_ctf, noise_inv)
        stacked = rolled_range(weighted, 0, ROT)
        cross = lax.dot_general(stacked, refs, (((1,), (1,)), ((), ())), preferred_element_type=jnp.float32)
        cross = cross.reshape(block, ROT, CLASSES)
        normal = jnp.dot(curve, power.T, precision=lax.Precision.HIGHEST)
        scores = cross - 0.5 * normal[:, None, :] - offset[:, None, None]
        post = jax.nn.softmax(scores.reshape(block, ROT * CLASSES), axis=1)
        post = post.reshape(block, ROT, CLASSES).astype(jnp.bfloat16)
        numer = numer + lax.dot_general(post.reshape(block * ROT, CLASSES), stacked, (((0,), (0,)), ((), ())), preferred_element_type=jnp.float32)
        mass = jnp.sum(post.astype(jnp.float32), axis=1)
        denom = denom + jnp.dot(mass.T, curve, precision=lax.Precision.HIGHEST)
        return (numer, denom), None

    start_carry = (jnp.zeros((CLASSES, PIX), jnp.float32), jnp.zeros((CLASSES, CYCLES), jnp.float32))
    (numer, denom), _ = lax.scan(one_block, start_carry, starts)
    bottom = denom + reg[None, :]
    return numer / jnp.tile(bottom, (1, 2 * ANGLES))
```

```python
import jax
import jax.numpy as jnp
from jax import lax
from jax.experimental import pallas as pl
from jax.experimental.pallas import tpu as pltpu
from jax.sharding import PartitionSpec as P

MESH = pl.DeviceIdType.MESH
BF16 = jnp.bfloat16
F32 = jnp.float32
HIGHEST = lax.Precision.HIGHEST

CYCLES = 64
ANGLES = 72
PIX = 9216
ROWS = 8
SLOTS = 8
PART = 64
HALF = 64
PAIRS = 36
WIDE = 256
TURN = 4
SHIFT = 9
PIECE = 16
QUARTER = PIX // 4
FULL = QUARTER + 256
CUT = FULL // 2


def ring(v, step):
    return lax.rem(v + step, 4)


def where_am_i():
    cls = lax.axis_index("cls")
    grp = lax.axis_index("grp")
    core = lax.rem(cls, 2)
    y_lo = lax.div(cls, 2)
    x = lax.div(grp, 8)
    y_hi = lax.rem(lax.div(grp, 4), 2)
    z = lax.rem(grp, 4)
    return x, y_hi, y_lo, z, core


def device(x, y, z, core):
    return (lax.rem(y, 2) * 2 + core, x * 8 + lax.div(y, 2) * 4 + z)


def dot_nt(a, b, precision=None):
    return lax.dot_general(a, b, (((1,), (1,)), ((), ())), precision=precision, preferred_element_type=F32)


def dot_nn(a, b, precision=None):
    return lax.dot_general(a, b, (((1,), (0,)), ((), ())), precision=precision, preferred_element_type=F32)


def twice(v):
    return jnp.concatenate([v, v], axis=1)


def split(v):
    high = v.astype(BF16)
    return high, (v - high.astype(F32)).astype(BF16)


def remote(src, dst, send, recv, target):
    return pltpu.make_async_remote_copy(
        src_ref=src, dst_ref=dst, send_sem=send, recv_sem=recv, device_id=target, device_id_type=MESH
    )


def expect(images, ctf, refs, noise, parts, gathered, ctfs, turned, classes, curves, squares, powers, cross,
           weights, numer, stats, own_stats, img_send, img_recv, ctf_send, ctf_recv, st_send, st_recv, loc_sem, ref_sem):
    x, y_hi, y_lo, z, core = where_am_i()
    y = y_hi * 2 + y_lo
    me = y * 2 + core
    up, down, far = ring(y, 1), ring(y, 3), ring(y, 2)

    first = pl.multiple_of(y_hi * HALF, HALF)
    ref_copies = []
    for b in range(PAIRS + SHIFT - 1):
        ref_copies.append(pltpu.make_async_copy(
            refs.at[pl.ds(first, HALF), pl.ds((b % PAIRS) * WIDE, WIDE)], classes.at[b], ref_sem.at[b]))
        ref_copies[-1].start()
    local = [
        pltpu.make_async_copy(images, gathered.at[me], loc_sem.at[0]),
        pltpu.make_async_copy(ctf, ctfs.at[me], loc_sem.at[1]),
    ]
    for copy in local:
        copy.start()

    def peer(o):
        slot = lax.rem(me + o, SLOTS)
        return device(x, lax.div(slot, 2), z, lax.rem(slot, 2))

    barrier = pltpu.get_barrier_semaphore()
    for o in range(1, SLOTS):
        pl.semaphore_signal(barrier, inc=1, device_id=peer(o), device_id_type=MESH)
    pl.semaphore_wait(barrier, SLOTS - 1)

    sibling = device(x, y, z, 1 - core)
    above = device(x, up, z, core)
    below = device(x, down, z, core)
    low = pl.ds(0, PIX // 2)
    high = pl.ds(PIX // 2, PIX // 2)
    slot_down, slot_up, slot_far = down * 2 + core, up * 2 + core, far * 2 + core

    def image(i, src, dst, target):
        return remote(src, dst, img_send.at[i], img_recv.at[i], target)

    whole = gathered.at[me]
    sends = [
        image(0, images, whole, above),
        image(1, images, whole, below),
        image(2, images, whole, sibling),
    ]
    sends[0].start()
    sends[1].start()
    ctf_copies = [remote(ctf, ctfs.at[me], ctf_send.at[o - 1], ctf_recv.at[o - 1], peer(o)) for o in range(1, SLOTS)]
    for copy in ctf_copies:
        copy.start()
    sends[2].start()

    for copy in ref_copies:
        copy.wait()

    powers[...] = jnp.zeros_like(powers)

    @pl.loop(0, PAIRS)
    def _(b):
        v = classes[b].astype(F32)
        v = v * v
        powers[...] += v[:, :128] + v[:, 128:]

    for copy in local:
        copy.wait()
    for copy in ctf_copies:
        copy.wait_recv()

    noise_row = noise[...]
    noise_wide = twice(noise_row)

    def prepare(level):
        rows = pl.ds(pl.multiple_of(level * 2 * ROWS, 2 * ROWS), 2 * ROWS)
        factors = []
        for c in range(2):
            value = ctfs[level * 2 + c].astype(F32)
            factor = value * noise_row
            curves[pl.ds(pl.multiple_of(level * 2 * ROWS + c * ROWS, ROWS), ROWS), :] = twice(factor * value)
            factors.append(twice(factor))
        sums = [jnp.zeros((ROWS, 128), F32) for c in range(2)]
        for a in range(ANGLES):
            lanes = pl.ds(a * 128, 128)
            out = []
            for c in range(2):
                value = gathered[level * 2 + c, :, lanes].astype(F32)
                sums[c] = sums[c] + value * value * noise_wide
                out.append(value * factors[c])
            block = jnp.concatenate(out, axis=0).astype(BF16)
            for t in range(TURN):
                place = (a * 128 - t * SHIFT * WIDE) % PIX
                turned[pl.ds(pl.multiple_of(t * PART + level * 2 * ROWS, 2 * ROWS), 2 * ROWS), pl.ds(place, 128)] = block
        squares[rows, :] = jnp.concatenate(sums, axis=0)

    sends[0].wait_recv()
    sends += [
        image(3, gathered.at[slot_down, :, low], gathered.at[slot_down, :, low], above),
        image(4, gathered.at[slot_down], gathered.at[slot_down], sibling),
    ]
    sends[3].start()
    sends[4].start()
    sends[1].wait_recv()
    sends += [
        image(5, gathered.at[slot_up, :, high], gathered.at[slot_up, :, high], below),
        image(6, gathered.at[slot_up], gathered.at[slot_up], sibling),
    ]
    sends[5].start()
    sends[6].start()
    sends[2].wait_recv()
    prepare(y)
    sends[3].wait_recv()
    sends.append(image(7, gathered.at[slot_far, :, low], gathered.at[slot_far, :, low], sibling))
    sends[7].start()
    sends[5].wait_recv()
    sends.append(image(8, gathered.at[slot_far, :, high], gathered.at[slot_far, :, high], sibling))
    sends[8].start()
    sends[4].wait_recv()
    prepare(down)
    sends[6].wait_recv()
    prepare(up)
    sends[7].wait_recv()
    sends[8].wait_recv()
    prepare(far)

    cross[...] = jnp.zeros_like(cross)

    @pl.loop(0, PAIRS // 4)
    def _(u):
        left = jnp.concatenate(
            [classes[pl.ds(u * 4 + v, SHIFT)].reshape(SHIFT * HALF, WIDE) for v in range(4)], axis=1)
        right = turned[:, pl.ds(pl.multiple_of(u * 4 * WIDE, 4 * WIDE), 4 * WIDE)]
        cross[...] += dot_nt(left, right)

    curve_rows = jnp.concatenate([curves[...]] * TURN, axis=0)
    square_rows = jnp.concatenate([squares[...]] * TURN, axis=0)
    normal = dot_nt(powers[...], curve_rows, HIGHEST)
    offset = 0.5 * dot_nt(jnp.ones((8, 128), F32), square_rows, HIGHEST)
    bias = 0.5 * normal + offset[:1, :]

    def over_turns(v, op):
        v = op(v, pltpu.roll(v, 64, 1))
        return op(v, pltpu.roll(v, 128, 1))

    top = None
    for s in range(SHIFT):
        value = cross[pl.ds(s * HALF, HALF), :] - bias
        cross[pl.ds(s * HALF, HALF), :] = value
        value = jnp.max(value, axis=0, keepdims=True)
        top = value if top is None else jnp.maximum(top, value)
    top = over_turns(jnp.broadcast_to(top, (8, WIDE)), jnp.maximum)
    total = None
    for s in range(SHIFT):
        value = jnp.exp(cross[pl.ds(s * HALF, HALF), :] - top[:1, :])
        cross[pl.ds(s * HALF, HALF), :] = value
        value = jnp.sum(value, axis=0, keepdims=True)
        total = value if total is None else total + value
    total = over_turns(jnp.broadcast_to(total, (8, WIDE)), jnp.add)
    own_stats[0] = top
    own_stats[1] = total

    stat_copies = [remote(own_stats, stats.at[o - 1], st_send.at[o - 1], st_recv.at[o - 1], peer(o)) for o in range(1, SLOTS)]
    for copy in stat_copies:
        copy.start()
    numer[...] = jnp.zeros_like(numer)
    for copy in stat_copies:
        copy.wait_recv()
    best = top
    for o in range(SLOTS - 1):
        best = jnp.maximum(best, stats[o, 0])
    mine = jnp.exp(top - best)
    norm = total * mine
    for o in range(SLOTS - 1):
        norm = norm + stats[o, 1] * jnp.exp(stats[o, 0] - best)
    scale = (mine / norm)[:1, :]

    mass = None
    for s in range(SHIFT):
        value = (cross[pl.ds(s * HALF, HALF), :] * scale).astype(BF16)
        weights[pl.ds(s * HALF, HALF), :] = value
        value = value.astype(F32)
        mass = value if mass is None else mass + value
    denom = dot_nn(mass, curve_rows, HIGHEST)
    denom_high, denom_low = split(denom)

    @pl.loop(0, PAIRS)
    def _(b):
        out = dot_nn(weights[...], turned[:, pl.ds(pl.multiple_of(b * WIDE, WIDE), WIDE)])
        for s in range(SHIFT):
            numer[b + s] += out[s * HALF:(s + 1) * HALF]

    for b in range(PAIRS):
        value = numer[b]
        if b < SHIFT - 1:
            value = value + numer[PAIRS + b]
        value = value.astype(BF16)
        for k in range(HALF // PIECE):
            parts[k, b // 9, :, pl.ds((b % 9) * WIDE, WIDE)] = value[k * PIECE:(k + 1) * PIECE]
    for k in range(HALF // PIECE):
        for q in range(4):
            parts[k, q, :, pl.ds(QUARTER, 128)] = denom_high[k * PIECE:(k + 1) * PIECE]
            parts[k, q, :, pl.ds(QUARTER + 128, 128)] = denom_low[k * PIECE:(k + 1) * PIECE]

    for copy in sends + ctf_copies + stat_copies:
        copy.wait_send()


def packed(v):
    size = v.shape[-1] - 256
    high, low = split(v[..., size:size + 128] + v[..., size + 128:])
    return jnp.concatenate([v[..., :size].astype(BF16), high, low], axis=-1)


def maximize(parts, reg, out, near_a, near_b, near_c, near_d, near_e, near_f, fwd_a, fwd_b, total, ready,
             two_a, two_b, two_c, two_d, two_e, two_f, two_fa, two_fb, rs_send, rs_recv, ag_send, ag_recv):
    x, y_hi, y_lo, z, core = where_am_i()
    y = y_hi * 2 + y_lo
    q1 = x + core * (z - x)
    q2 = z + core * (x - z)

    def at(v1, v2):
        return device(v1 + core * (v2 - v1), y, v2 + core * (v1 - v2), core)

    right1, left1, opp1 = ring(q1, 1), ring(q1, 3), ring(q1, 2)
    right2, left2, opp2 = ring(q2, 1), ring(q2, 3), ring(q2, 2)
    to_r1, to_l1 = at(right1, q2), at(left1, q2)
    to_r2, to_l2 = at(q1, right2), at(q1, left2)
    to_y = device(x, ring(y, 2), z, core)

    barrier = pltpu.get_barrier_semaphore()
    for target in (to_r1, to_l1, to_r2, to_l2, to_y):
        pl.semaphore_signal(barrier, inc=1, device_id=target, device_id_type=MESH)
    pl.semaphore_wait(barrier, 5)

    def reduce_copy(i, src, dst, target):
        copy = remote(src, dst, rs_send.at[i], rs_recv.at[i], target)
        copy.start()
        return copy

    low, high = pl.ds(0, 2), pl.ds(2, 2)
    a = reduce_copy(0, parts.at[opp1, low], near_a, to_r1)
    b = reduce_copy(1, parts.at[opp1, high], near_b, to_l1)
    c = reduce_copy(2, parts.at[right1, high], near_c, to_r1)
    d = reduce_copy(3, parts.at[left1, low], near_d, to_l1)
    a.wait_recv()
    fwd_a[...] = packed(parts[right1, low].astype(F32) + near_a[...].astype(F32))
    e = reduce_copy(4, fwd_a, near_e, to_r1)
    b.wait_recv()
    fwd_b[...] = packed(parts[left1, high].astype(F32) + near_b[...].astype(F32))
    f = reduce_copy(5, fwd_b, near_f, to_l1)
    d.wait_recv()
    e.wait_recv()
    total[low] = parts[q1, low].astype(F32) + near_d[...].astype(F32) + near_e[...].astype(F32)
    c.wait_recv()
    f.wait_recv()
    total[high] = parts[q1, high].astype(F32) + near_c[...].astype(F32) + near_f[...].astype(F32)
    ready[...] = packed(total[...])

    left, right = pl.ds(0, CUT), pl.ds(CUT, CUT)
    a2 = reduce_copy(6, ready.at[opp2, :, left], two_a, to_r2)
    b2 = reduce_copy(7, ready.at[opp2, :, right], two_b, to_l2)
    c2 = reduce_copy(8, ready.at[right2, :, right], two_c, to_r2)
    d2 = reduce_copy(9, ready.at[left2, :, left], two_d, to_l2)
    a2.wait_recv()
    two_fa[...] = (total[right2, :, left] + two_a[...].astype(F32)).astype(BF16)
    e2 = reduce_copy(10, two_fa, two_e, to_r2)
    b2.wait_recv()
    two_fb[...] = packed(total[left2, :, right] + two_b[...].astype(F32))
    f2 = reduce_copy(11, two_fb, two_f, to_l2)
    d2.wait_recv()
    e2.wait_recv()
    first = total[q2, :, left] + two_d[...].astype(F32) + two_e[...].astype(F32)
    c2.wait_recv()
    f2.wait_recv()
    second = total[q2, :, right] + two_c[...].astype(F32) + two_f[...].astype(F32)
    size = QUARTER - CUT
    bottom = second[:, size:size + 128] + second[:, size + 128:] + twice(reg[...])
    numer = jnp.concatenate([first, second[:, :size]], axis=1)

    def block(half, v1, v2, start=0, count=QUARTER):
        level = y_hi if half == 0 else 1 - y_hi
        return out.at[pl.ds(pl.multiple_of(level * HALF + v1 * PIECE, PIECE), PIECE),
                      pl.ds(pl.multiple_of(v2 * QUARTER + start, 128), count)]

    own = block(0, q1, q2)
    own[...] = (numer / jnp.concatenate([bottom] * (QUARTER // 128), axis=1)).astype(BF16)

    copies = {}

    def gather(name, half, v1, v2, target, start=0, count=QUARTER):
        ref = block(half, v1, v2, start, count)
        i = len(copies)
        copies[name] = remote(ref, ref, ag_send.at[i], ag_recv.at[i], target)
        copies[name].start()

    def arrived(*names):
        for name in names:
            copies[name].wait_recv()

    mid = QUARTER // 2

    def spread(half, j, v2):
        gather((half, "right", j), half, q1, v2, to_r1)
        gather((half, "left", j), half, q1, v2, to_l1)

    def begin(half):
        gather((half, "r2"), half, q1, q2, to_r2)
        gather((half, "l2"), half, q1, q2, to_l2)
        spread(half, 0, q2)

    def middle(half):
        arrived((half, "r2"))
        gather((half, "fr2"), half, q1, left2, to_r2, 0, mid)
        spread(half, 1, left2)
        arrived((half, "l2"))
        gather((half, "fl2"), half, q1, right2, to_l2, mid, mid)
        spread(half, 2, right2)

    def last(half):
        arrived((half, "fr2"), (half, "fl2"))
        spread(half, 3, opp2)

    def relay(half, j, v2):
        arrived((half, "right", j), (half, "left", j))
        if j in (0, 3):
            gather((half, "fright", j), half, left1, v2, to_r1)
        else:
            gather((half, "fleft", j), half, right1, v2, to_l1)

    gather("y", 0, q1, q2, to_y)
    begin(0)
    middle(0)
    arrived("y")
    begin(1)
    last(0)
    relay(0, 0, q2)
    middle(1)
    relay(0, 1, left2)
    relay(0, 2, right2)
    last(1)
    relay(0, 3, opp2)
    relay(1, 0, q2)
    relay(1, 1, left2)
    relay(1, 2, right2)
    relay(1, 3, opp2)
    for half in (0, 1):
        arrived((half, "fright", 0), (half, "fright", 3), (half, "fleft", 1), (half, "fleft", 2))
    for copy in [a, b, c, d, e, f, a2, b2, c2, d2, e2, f2] + list(copies.values()):
        copy.wait_send()


def body(images, ctf, refs, noise_inv, reg):
    any_space = pl.BlockSpec(memory_space=pl.ANY)
    vmem = pl.BlockSpec(memory_space=pltpu.VMEM)
    dma = pltpu.SemaphoreType.DMA
    parts = pl.pallas_call(
        expect,
        out_shape=jax.ShapeDtypeStruct((4, 4, PIECE, FULL), BF16),
        in_specs=[any_space, any_space, any_space, vmem],
        out_specs=vmem,
        scratch_shapes=[
            pltpu.VMEM((SLOTS, ROWS, PIX), BF16),
            pltpu.VMEM((SLOTS, ROWS, CYCLES), BF16),
            pltpu.VMEM((TURN * PART, PIX), BF16),
            pltpu.VMEM((PAIRS + SHIFT - 1, HALF, WIDE), BF16),
            pltpu.VMEM((PART, 128), F32),
            pltpu.VMEM((PART, 128), F32),
            pltpu.VMEM((HALF, 128), F32),
            pltpu.VMEM((SHIFT * HALF, TURN * PART), F32),
            pltpu.VMEM((SHIFT * HALF, TURN * PART), BF16),
            pltpu.VMEM((PAIRS + SHIFT - 1, HALF, WIDE), F32),
            pltpu.VMEM((SLOTS - 1, 2, 8, WIDE), F32),
            pltpu.VMEM((2, 8, WIDE), F32),
            dma((9,)), dma((9,)), dma((7,)), dma((7,)), dma((7,)), dma((7,)), dma((2,)),
            dma((PAIRS + SHIFT - 1,)),
        ],
        compiler_params=pltpu.CompilerParams(
            collective_id=0, has_side_effects=True, vmem_limit_bytes=40 * 1024 * 1024),
        name="expect",
    )(images, ctf, refs, noise_inv.reshape(1, CYCLES))
    near = pltpu.VMEM((2, PIECE, FULL), BF16)
    two = pltpu.VMEM((PIECE, CUT), BF16)
    result = pl.pallas_call(
        maximize,
        out_shape=jax.ShapeDtypeStruct((2 * HALF, PIX), BF16),
        in_specs=[vmem, vmem],
        out_specs=vmem,
        scratch_shapes=[near] * 8 + [
            pltpu.VMEM((4, PIECE, FULL), F32),
            pltpu.VMEM((4, PIECE, FULL), BF16),
        ] + [two] * 8 + [dma((12,)), dma((12,)), dma((33,)), dma((33,))],
        compiler_params=pltpu.CompilerParams(
            collective_id=1, has_side_effects=True, vmem_limit_bytes=24 * 1024 * 1024),
        name="maximize",
    )(parts, reg.reshape(1, CYCLES))
    return result.astype(F32)


def solution(mesh):
    in_specs = (P(("cls", "grp"), None), P(("cls", "grp"), None), P("cls", None), P(), P())
    return jax.shard_map(body, mesh=mesh, in_specs=in_specs, out_specs=P("cls", None), check_vma=False)
```

```python
import jax
import jax.numpy as jnp
from jax import lax
from jax.experimental import pallas as pl
from jax.experimental.pallas import tpu as pltpu
from jax.sharding import PartitionSpec as P

MESH = pl.DeviceIdType.MESH
BF16 = jnp.bfloat16
F32 = jnp.float32
HIGHEST = lax.Precision.HIGHEST

CYCLES = 64
PIX = 9216
ROWS = 8
SLOTS = 8
PART = 64
HALF = 64
BLOCKS = 36
WIDE = 256
TURN = 4
SHIFT = 9
PIECE = 16
QUARTER = PIX // 4
FULL = QUARTER + 256
CUT = FULL // 2
CHUNKS = 3
CHUNK = PIX // CHUNKS
PER = BLOCKS // CHUNKS
STEP = 3


def ring(v, step):
    return lax.rem(v + step, 4)


def device(x, y, z, core):
    return (lax.rem(y, 2) * 2 + core, x * 8 + lax.div(y, 2) * 4 + z)


def dot_nt(a, b, precision=None):
    return lax.dot_general(a, b, (((1,), (1,)), ((), ())), precision=precision, preferred_element_type=F32)


def dot_nn(a, b, precision=None):
    return lax.dot_general(a, b, (((1,), (0,)), ((), ())), precision=precision, preferred_element_type=F32)


def twice(v):
    return jnp.concatenate([v, v], axis=1)


def split(v):
    high = v.astype(BF16)
    return high, (v - high.astype(F32)).astype(BF16)


def remote(src, dst, send, recv, target):
    return pltpu.make_async_remote_copy(
        src_ref=src, dst_ref=dst, send_sem=send, recv_sem=recv, device_id=target, device_id_type=MESH
    )


def kernel(images, ctf, refs, noise_hbm, reg_hbm, out, gathered, ctfs, blocks, classes, noise, reg, factors, curves,
           squares, powers, cross, weights, stats, own_stats, numer, bottoms, parts, far_low, far_high, plain, summed,
           fwd, total, total_bottom, ready, two_a, two_b, two_c, two_d, two_e, two_f, two_fa, two_fb, pieces,
           img_send, img_recv, ctf_send, ctf_recv, st_send, st_recv, loc_sem, ref_sem, rs_send, rs_recv, ag_send, ag_recv):
    cls = lax.axis_index("cls")
    grp = lax.axis_index("grp")
    core = lax.rem(cls, 2)
    x = lax.div(grp, 8)
    z = lax.rem(grp, 4)
    y_hi = lax.rem(lax.div(grp, 4), 2)
    y = y_hi * 2 + lax.div(cls, 2)
    me = y * 2 + core
    up, down, far = ring(y, 1), ring(y, 3), ring(y, 2)
    q1 = x + core * (z - x)
    q2 = z + core * (x - z)

    def at(v1, v2):
        return device(v1 + core * (v2 - v1), y, v2 + core * (v1 - v2), core)

    right1, left1, opp1 = ring(q1, 1), ring(q1, 3), ring(q1, 2)
    right2, left2, opp2 = ring(q2, 1), ring(q2, 3), ring(q2, 2)
    to_r1, to_l1 = at(right1, q2), at(left1, q2)
    to_r2, to_l2 = at(q1, right2), at(q1, left2)
    to_y = device(x, far, z, core)

    def peer(o):
        slot = lax.rem(me + o, SLOTS)
        return device(x, lax.div(slot, 2), z, lax.rem(slot, 2))

    barrier = pltpu.get_barrier_semaphore()
    for o in range(1, SLOTS):
        pl.semaphore_signal(barrier, inc=1, device_id=peer(o), device_id_type=MESH)
    for target in (to_r1, to_l1, to_r2, to_l2):
        pl.semaphore_signal(barrier, inc=1, device_id=target, device_id_type=MESH)

    local = [
        pltpu.make_async_copy(images, gathered.at[me], loc_sem.at[0]),
        pltpu.make_async_copy(ctf, ctfs.at[me], loc_sem.at[1]),
        pltpu.make_async_copy(noise_hbm, noise, loc_sem.at[2]),
        pltpu.make_async_copy(reg_hbm, reg, loc_sem.at[3]),
    ]
    for copy in local:
        copy.start()
    first = pl.multiple_of(y_hi * HALF, HALF)
    ref_copies = []
    for j in range(4):
        for m in range(2 * SHIFT - 1):
            b = (4 * m + j) % BLOCKS
            ref_copies.append(pltpu.make_async_copy(
                refs.at[pl.ds(first, HALF), pl.ds(b * WIDE, WIDE)], classes.at[j, m], ref_sem.at[len(ref_copies)]))
            ref_copies[-1].start()

    pl.semaphore_wait(barrier, SLOTS + 3)

    sibling = device(x, y, z, 1 - core)
    above = device(x, up, z, core)
    below = device(x, down, z, core)
    slot_down, slot_up, slot_far = down * 2 + core, up * 2 + core, far * 2 + core
    moves = {}

    def move(c, i):
        if i < 3:
            slot, lo, size, target = me, 0, CHUNK, (above, below, sibling)[i]
        elif i == 3:
            slot, lo, size, target = slot_down, 0, CHUNK // 2, above
        elif i == 4:
            slot, lo, size, target = slot_down, 0, CHUNK, sibling
        elif i == 5:
            slot, lo, size, target = slot_up, CHUNK // 2, CHUNK // 2, below
        elif i == 6:
            slot, lo, size, target = slot_up, 0, CHUNK, sibling
        else:
            slot, lo, size, target = slot_far, (i - 7) * (CHUNK // 2), CHUNK // 2, sibling
        lanes = pl.ds(c * CHUNK + lo, size)
        src = images.at[:, lanes] if i < 3 else gathered.at[slot, :, lanes]
        moves[c, i] = remote(src, gathered.at[slot, :, lanes], img_send.at[9 * c + i], img_recv.at[9 * c + i], target)
        moves[c, i].start()

    def neighbours(c):
        moves[c, 0].wait_recv()
        move(c, 3)
        move(c, 4)
        moves[c, 1].wait_recv()
        move(c, 5)
        move(c, 6)

    def distant(c):
        moves[c, 3].wait_recv()
        move(c, 7)
        moves[c, 5].wait_recv()
        move(c, 8)

    def complete(c):
        for i in (2, 4, 6, 7, 8):
            moves[c, i].wait_recv()

    move(0, 0)
    move(0, 1)
    move(1, 0)
    move(1, 1)
    ctf_copies = [remote(ctf, ctfs.at[me], ctf_send.at[o - 1], ctf_recv.at[o - 1], peer(o)) for o in range(1, SLOTS)]
    for copy in ctf_copies:
        copy.start()
    move(0, 2)
    cross[...] = jnp.zeros_like(cross)
    squares[...] = jnp.zeros_like(squares)
    for copy in local:
        copy.wait()
    neighbours(0)
    move(2, 0)
    move(2, 1)
    move(1, 2)
    move(2, 2)
    for copy in ref_copies:
        copy.wait()
    powers[...] = jnp.zeros_like(powers)

    @pl.loop(0, SHIFT)
    def _(m):
        value = powers[...]
        for j in range(4):
            v = classes[j, m].astype(F32)
            v = v * v
            value = value + (v[:, :128] + v[:, 128:])
        powers[...] = value

    for copy in ctf_copies:
        copy.wait_recv()
    noise_row = noise[...]
    for slot in range(SLOTS):
        value = ctfs[slot].astype(F32)
        factor = value * noise_row
        factors[pl.ds(slot * ROWS, ROWS), :] = twice(factor)
        curves[pl.ds(slot * ROWS, ROWS), :] = twice(factor * value)

    def prepare(c):
        @pl.loop(c * PER, (c + 1) * PER)
        def _(b):
            lanes = pl.ds(pl.multiple_of(b * WIDE, WIDE), WIDE)
            for level in range(4):
                weighted = []
                for core_slot in range(2):
                    slot = level * 2 + core_slot
                    rows = pl.ds(slot * ROWS, ROWS)
                    value = gathered[slot, :, lanes].astype(F32)
                    square = value * value
                    squares[rows, :] += square[:, :128] + square[:, 128:]
                    weighted.append(value * twice(factors[rows, :]))
                blocks[b, pl.ds(level * 2 * ROWS, 2 * ROWS), :] = jnp.concatenate(weighted, axis=0).astype(BF16)

    def score(start, stop):
        @pl.loop(start // STEP, stop // STEP)
        def _(u):
            left, right = [], []
            for v in range(STEP):
                b = u * STEP + v
                left.append(classes[lax.rem(b, 4), pl.ds(lax.div(b, 4), SHIFT)].reshape(SHIFT * HALF, WIDE))
                right.append(blocks[pl.ds(b, TURN)].reshape(TURN * PART, WIDE))
            cross[...] += dot_nt(jnp.concatenate(left, axis=1), jnp.concatenate(right, axis=1))

    neighbours(1)
    distant(0)
    complete(0)
    neighbours(2)
    distant(1)
    prepare(0)
    for t in range(TURN - 1):
        blocks[BLOCKS + t] = blocks[t]
    score(0, PER - STEP)
    distant(2)
    complete(1)
    prepare(1)
    score(PER - STEP, 2 * PER - STEP)
    complete(2)
    prepare(2)
    score(2 * PER - STEP, BLOCKS)

    curve_rows = jnp.concatenate([curves[...]] * TURN, axis=0)
    square_rows = jnp.concatenate([squares[...] * twice(noise_row)] * TURN, axis=0)
    normal = dot_nt(powers[...], curve_rows, HIGHEST)
    offset = 0.5 * dot_nt(jnp.ones((8, 128), F32), square_rows, HIGHEST)
    bias = 0.5 * normal + offset[:1, :]

    def over_turns(v, op):
        v = op(v, pltpu.roll(v, 64, 1))
        return op(v, pltpu.roll(v, 128, 1))

    top = None
    for s in range(SHIFT):
        value = cross[pl.ds(s * HALF, HALF), :] - bias
        cross[pl.ds(s * HALF, HALF), :] = value
        value = jnp.max(value, axis=0, keepdims=True)
        top = value if top is None else jnp.maximum(top, value)
    top = over_turns(jnp.broadcast_to(top, (8, WIDE)), jnp.maximum)
    norm = None
    for s in range(SHIFT):
        value = jnp.exp(cross[pl.ds(s * HALF, HALF), :] - top[:1, :])
        cross[pl.ds(s * HALF, HALF), :] = value
        value = jnp.sum(value, axis=0, keepdims=True)
        norm = value if norm is None else norm + value
    norm = over_turns(jnp.broadcast_to(norm, (8, WIDE)), jnp.add)
    row = lax.broadcasted_iota(jnp.int32, (8, WIDE), 0)
    own_stats[...] = jnp.where(row < 4, top, norm)

    stat_copies = [remote(own_stats, stats.at[o - 1], st_send.at[o - 1], st_recv.at[o - 1], peer(o)) for o in range(1, SLOTS)]
    for copy in stat_copies:
        copy.start()
    for copy in stat_copies:
        copy.wait_recv()
    top, norm = top[:1, :], norm[:1, :]
    best = top
    for o in range(SLOTS - 1):
        best = jnp.maximum(best, stats[o, 0:1, :])
    mine = jnp.exp(top - best)
    norm = norm * mine
    for o in range(SLOTS - 1):
        norm = norm + stats[o, 4:5, :] * jnp.exp(stats[o, 0:1, :] - best)
    scale = mine / norm

    mass = None
    for s in range(SHIFT):
        value = (cross[pl.ds(s * HALF, HALF), :] * scale).astype(BF16)
        weights[pl.ds(s * HALF, HALF), :] = value
        value = value.astype(F32)
        mass = value if mass is None else mass + value
    denom = dot_nn(mass, curve_rows, HIGHEST)
    for k in range(4):
        bottoms[k] = denom[k * PIECE:(k + 1) * PIECE]

    def accumulate(j):
        for m in range(SHIFT):
            value = dot_nn(weights[...], blocks[pl.ds(4 * m + j, TURN)].reshape(TURN * PART, WIDE))
            for s in range(SHIFT):
                piece = value[s * HALF:(s + 1) * HALF]
                if m == 0:
                    numer[j, s] = piece
                else:
                    numer[j, (m + s) % SHIFT] += piece

    def lanes(m):
        return pl.ds(m * WIDE, WIDE)

    ends = pl.ds(QUARTER, 128), pl.ds(QUARTER + 128, 128)

    def finish_ends(ref, index, value):
        high, low = split(value)
        ref[index, :, ends[0]] = high
        ref[index, :, ends[1]] = low

    def read_ends(ref, index):
        return ref[index, :, ends[0]].astype(F32) + ref[index, :, ends[1]].astype(F32)

    def pack(j, ks):
        for k in ks:
            for m in range(SHIFT):
                parts[j, k, :, lanes(m)] = numer[j, m, pl.ds(k * PIECE, PIECE), :].astype(BF16)
            high, low = split(bottoms[k])
            parts[j, k, :, ends[0]] = high
            parts[j, k, :, ends[1]] = low

    def pass_on(j, ks, near):
        for k in ks:
            for m in range(SHIFT):
                fwd[k, :, lanes(m)] = (
                    numer[j, m, pl.ds(k * PIECE, PIECE), :] + near[k - ks[0], :, lanes(m)].astype(F32)).astype(BF16)
            finish_ends(fwd, k, bottoms[k] + read_ends(near, k - ks[0]))

    reduced = []

    def reduce_copy(src, dst, target):
        i = len(reduced)
        reduced.append(remote(src, dst, rs_send.at[i], rs_recv.at[i], target))
        reduced[i].start()
        return reduced[i]

    low, high = pl.ds(0, 2), pl.ds(2, 2)
    accumulate(opp1)
    pack(opp1, range(4))
    a = reduce_copy(parts.at[opp1, low], far_low, to_r1)
    b = reduce_copy(parts.at[opp1, high], far_high, to_l1)
    accumulate(right1)
    pack(right1, (2, 3))
    c = reduce_copy(parts.at[right1, high], plain.at[high], to_r1)
    accumulate(left1)
    pack(left1, (0, 1))
    d = reduce_copy(parts.at[left1, low], plain.at[low], to_l1)
    a.wait_recv()
    pass_on(right1, (0, 1), far_low)
    e = reduce_copy(fwd.at[low], summed.at[low], to_r1)
    b.wait_recv()
    pass_on(left1, (2, 3), far_high)
    f = reduce_copy(fwd.at[high], summed.at[high], to_l1)
    accumulate(q1)
    for copy in (c, d, e, f):
        copy.wait_recv()

    def settle(k):
        rows = pl.ds(pl.multiple_of(k * PIECE, PIECE), PIECE)
        for m in range(SHIFT):
            value = (numer[q1, m, rows, :] + plain[k, :, lanes(m)].astype(F32)) + summed[k, :, lanes(m)].astype(F32)
            total[k, :, lanes(m)] = value
            ready[k, :, lanes(m)] = value.astype(BF16)
        value = bottoms[k] + read_ends(plain, k) + read_ends(summed, k)
        total_bottom[k] = value
        finish_ends(ready, k, value)

    left, right = pl.ds(0, CUT), pl.ds(CUT, CUT)
    rest = QUARTER - CUT
    settle(opp2)
    a2 = reduce_copy(ready.at[opp2, :, left], two_a, to_r2)
    b2 = reduce_copy(ready.at[opp2, :, right], two_b, to_l2)
    settle(right2)
    c2 = reduce_copy(ready.at[right2, :, right], two_c, to_r2)
    settle(left2)
    d2 = reduce_copy(ready.at[left2, :, left], two_d, to_l2)
    settle(q2)

    def bottom_of(ref):
        return ref[:, pl.ds(rest, 128)].astype(F32) + ref[:, pl.ds(rest + 128, 128)].astype(F32)

    a2.wait_recv()
    two_fa[...] = (total[right2, :, left] + two_a[...].astype(F32)).astype(BF16)
    e2 = reduce_copy(two_fa, two_e, to_r2)
    b2.wait_recv()
    two_fb[:, pl.ds(0, rest)] = (total[left2, :, pl.ds(CUT, rest)] + two_b[:, pl.ds(0, rest)].astype(F32)).astype(BF16)
    hi, lo = split(total_bottom[left2] + bottom_of(two_b))
    two_fb[:, pl.ds(rest, 128)] = hi
    two_fb[:, pl.ds(rest + 128, 128)] = lo
    f2 = reduce_copy(two_fb, two_f, to_l2)
    for copy in (c2, d2, f2, e2):
        copy.wait_recv()
    inverse_rows = (total_bottom[q2] + bottom_of(two_c)) + bottom_of(two_f) + twice(reg[...])
    first_part = total[q2, :, left] + two_d[...].astype(F32) + two_e[...].astype(F32)
    second_part = (total[q2, :, pl.ds(CUT, rest)] + two_c[:, pl.ds(0, rest)].astype(F32)
                   + two_f[:, pl.ds(0, rest)].astype(F32))
    value = jnp.concatenate([first_part, second_part], axis=1)

    def level_of(half):
        return y_hi if half == 0 else 1 - y_hi

    def block(half, v1, v2, start=0, count=QUARTER):
        return pieces.at[level_of(half) * 4 + v2, v1, :, pl.ds(start, count)]

    pieces[y_hi * 4 + q2, q1] = (value / jnp.concatenate([inverse_rows] * (QUARTER // 128), axis=1)).astype(BF16)

    def deliver(half, v1, v2):
        index = level_of(half) * 4 + v2
        rows = pl.ds(pl.multiple_of(index * PIECE, PIECE), PIECE)
        for m in range(SHIFT):
            place = pl.ds(pl.multiple_of(v1 * WIDE + m * 4 * WIDE, WIDE), WIDE)
            out[rows, place] = pieces[index, v1, :, lanes(m)].astype(F32)

    copies = {}

    def gather(name, half, v1, v2, target, start=0, count=QUARTER):
        ref = block(half, v1, v2, start, count)
        i = len(copies)
        copies[name] = remote(ref, ref, ag_send.at[i], ag_recv.at[i], target)
        copies[name].start()

    def arrived(*names):
        for name in names:
            copies[name].wait_recv()

    mid = QUARTER // 2

    def spread(half, i, v2):
        gather((half, "right", i), half, q1, v2, to_r1)
        gather((half, "left", i), half, q1, v2, to_l1)

    def begin(half):
        gather((half, "r2"), half, q1, q2, to_r2)
        gather((half, "l2"), half, q1, q2, to_l2)
        spread(half, 0, q2)
        deliver(half, q1, q2)

    def middle(half):
        arrived((half, "r2"))
        gather((half, "fr2"), half, q1, left2, to_r2, 0, mid)
        spread(half, 1, left2)
        arrived((half, "l2"))
        gather((half, "fl2"), half, q1, right2, to_l2, mid, mid)
        spread(half, 2, right2)
        deliver(half, q1, left2)
        deliver(half, q1, right2)

    def last(half):
        arrived((half, "fr2"), (half, "fl2"))
        spread(half, 3, opp2)
        deliver(half, q1, opp2)

    def relay(half, i, v2):
        arrived((half, "right", i), (half, "left", i))
        if i in (0, 3):
            gather((half, "fright", i), half, left1, v2, to_r1)
        else:
            gather((half, "fleft", i), half, right1, v2, to_l1)
        deliver(half, left1, v2)
        deliver(half, right1, v2)

    gather("y", 0, q1, q2, to_y)
    begin(0)
    middle(0)
    arrived("y")
    begin(1)
    last(0)
    relay(0, 0, q2)
    middle(1)
    relay(0, 1, left2)
    relay(0, 2, right2)
    last(1)
    relay(0, 3, opp2)
    relay(1, 0, q2)
    relay(1, 1, left2)
    relay(1, 2, right2)
    relay(1, 3, opp2)
    for half in (0, 1):
        for i, v2, way in ((0, q2, "fright"), (1, left2, "fleft"), (2, right2, "fleft"), (3, opp2, "fright")):
            arrived((half, way, i))
            deliver(half, opp1, v2)
    for copy in list(moves.values()) + ctf_copies + stat_copies + reduced + list(copies.values()):
        copy.wait_send()


def body(images, ctf, refs, noise_inv, reg):
    hbm = pl.BlockSpec(memory_space=pltpu.MemorySpace.HBM)
    dma = pltpu.SemaphoreType.DMA
    vmem = pltpu.VMEM
    near = vmem((2, PIECE, FULL), BF16)
    four = vmem((4, PIECE, FULL), BF16)
    two = vmem((PIECE, CUT), BF16)
    return pl.pallas_call(
        kernel,
        out_shape=jax.ShapeDtypeStruct((2 * HALF, PIX), F32),
        in_specs=[hbm] * 5,
        out_specs=pl.BlockSpec(memory_space=pltpu.VMEM),
        scratch_shapes=[
            vmem((SLOTS, ROWS, PIX), BF16),
            vmem((SLOTS, ROWS, CYCLES), BF16),
            vmem((BLOCKS + TURN - 1, PART, WIDE), BF16),
            vmem((4, 2 * SHIFT - 1, HALF, WIDE), BF16),
            vmem((1, CYCLES), F32),
            vmem((1, CYCLES), F32),
            vmem((PART, 128), F32),
            vmem((PART, 128), F32),
            vmem((PART, 128), F32),
            vmem((HALF, 128), F32),
            vmem((SHIFT * HALF, TURN * PART), F32),
            vmem((SHIFT * HALF, TURN * PART), BF16),
            vmem((SLOTS - 1, 8, WIDE), F32),
            vmem((8, WIDE), F32),
            vmem((4, SHIFT, HALF, WIDE), F32),
            vmem((4, PIECE, 128), F32),
            vmem((4, 4, PIECE, FULL), BF16),
            near, near, four, four, four,
            vmem((4, PIECE, QUARTER), F32),
            vmem((4, PIECE, 128), F32),
            four,
            two, two, two, two, two, two, two, two,
            vmem((8, 4, PIECE, QUARTER), BF16),
            dma((9 * CHUNKS,)), dma((9 * CHUNKS,)), dma((7,)), dma((7,)), dma((7,)), dma((7,)), dma((4,)),
            dma((4 * (2 * SHIFT - 1),)), dma((12,)), dma((12,)), dma((33,)), dma((33,)),
        ],
        compiler_params=pltpu.CompilerParams(
            collective_id=0, has_side_effects=True, vmem_limit_bytes=40 * 1024 * 1024),
        name="step",
    )(images, ctf, refs, noise_inv.reshape(1, CYCLES), reg.reshape(1, CYCLES))


def solution(mesh):
    in_specs = (P(("cls", "grp"), None), P(("cls", "grp"), None), P("cls", None), P(), P())
    return jax.shard_map(body, mesh=mesh, in_specs=in_specs, out_specs=P("cls", None), check_vma=False)
```

```python
import jax
import jax.numpy as jnp
from jax import lax
from jax.experimental import pallas as pl
from jax.experimental.pallas import tpu as pltpu
from jax.sharding import PartitionSpec as P

MESH = pl.DeviceIdType.MESH
BF16 = jnp.bfloat16
F32 = jnp.float32
HIGHEST = lax.Precision.HIGHEST

CYCLES = 64
PIX = 9216
ROWS = 8
SLOTS = 8
PART = 64
HALF = 64
BLOCKS = 36
WIDE = 256
TURN = 4
SHIFT = 9
PIECE = 16
QUARTER = PIX // 4
FULL = QUARTER + 256
CHUNKS = 3
CHUNK = PIX // CHUNKS
PER = BLOCKS // CHUNKS
STEP = 4


def ring(v, step):
    return lax.rem(v + step, 4)


def device(x, y, z, core):
    return (lax.rem(y, 2) * 2 + core, x * 8 + lax.div(y, 2) * 4 + z)


def dot_nt(a, b, precision=None):
    return lax.dot_general(a, b, (((1,), (1,)), ((), ())), precision=precision, preferred_element_type=F32)


def dot_nn(a, b, precision=None):
    return lax.dot_general(a, b, (((1,), (0,)), ((), ())), precision=precision, preferred_element_type=F32)


def twice(v):
    return jnp.concatenate([v, v], axis=1)


def split(v):
    high = v.astype(BF16)
    return high, (v - high.astype(F32)).astype(BF16)


def remote(src, dst, send, recv, target):
    return pltpu.make_async_remote_copy(
        src_ref=src, dst_ref=dst, send_sem=send, recv_sem=recv, device_id=target, device_id_type=MESH
    )


def kernel(images, ctf, refs, noise_hbm, reg_hbm, out, gathered, ctfs, blocks, classes, noise, reg, factors, curves,
           squares, powers, cross, weights, stats, own_stats, numer, bottoms, parts, far_low, far_high, plain, summed,
           fwd, total, total_bottom, ready, two_left, two_right, two_far, pieces,
           img_send, img_recv, ctf_send, ctf_recv, st_send, st_recv, loc_sem, ref_sem, rs_send, rs_recv, ag_send, ag_recv):
    cls = lax.axis_index("cls")
    grp = lax.axis_index("grp")
    core = lax.rem(cls, 2)
    x = lax.div(grp, 8)
    z = lax.rem(grp, 4)
    y_hi = lax.rem(lax.div(grp, 4), 2)
    y = y_hi * 2 + lax.div(cls, 2)
    me = y * 2 + core
    up, down, far = ring(y, 1), ring(y, 3), ring(y, 2)
    q1 = x + core * (z - x)
    q2 = z + core * (x - z)

    def at(v1, v2):
        return device(v1 + core * (v2 - v1), y, v2 + core * (v1 - v2), core)

    right1, left1, opp1 = ring(q1, 1), ring(q1, 3), ring(q1, 2)
    right2, left2, opp2 = ring(q2, 1), ring(q2, 3), ring(q2, 2)
    to_r1, to_l1 = at(right1, q2), at(left1, q2)
    to_r2, to_l2 = at(q1, right2), at(q1, left2)
    to_o1, to_o2 = at(opp1, q2), at(q1, opp2)
    to_y = device(x, far, z, core)

    def peer(o):
        slot = lax.rem(me + o, SLOTS)
        return device(x, lax.div(slot, 2), z, lax.rem(slot, 2))

    barrier = pltpu.get_barrier_semaphore()
    for o in range(1, SLOTS):
        pl.semaphore_signal(barrier, inc=1, device_id=peer(o), device_id_type=MESH)
    for target in (to_r1, to_l1, to_o1, to_r2, to_l2, to_o2):
        pl.semaphore_signal(barrier, inc=1, device_id=target, device_id_type=MESH)

    local = [
        pltpu.make_async_copy(images, gathered.at[me], loc_sem.at[0]),
        pltpu.make_async_copy(ctf, ctfs.at[me], loc_sem.at[1]),
        pltpu.make_async_copy(noise_hbm, noise, loc_sem.at[2]),
        pltpu.make_async_copy(reg_hbm, reg, loc_sem.at[3]),
    ]
    for copy in local:
        copy.start()
    first = pl.multiple_of(y_hi * HALF, HALF)
    ref_copies = []
    for j in range(4):
        for m in range(2 * SHIFT - 1):
            b = (4 * m + j) % BLOCKS
            ref_copies.append(pltpu.make_async_copy(
                refs.at[pl.ds(first, HALF), pl.ds(b * WIDE, WIDE)], classes.at[j, m], ref_sem.at[len(ref_copies)]))
            ref_copies[-1].start()

    pl.semaphore_wait(barrier, SLOTS + 5)

    sibling = device(x, y, z, 1 - core)
    above = device(x, up, z, core)
    below = device(x, down, z, core)
    farthest = device(x, far, z, core)
    slot_down, slot_up, slot_far = down * 2 + core, up * 2 + core, far * 2 + core
    moves = {}

    def move(c, i):
        slot = (me, me, me, me, slot_far, slot_down, slot_up)[i]
        target = (farthest, above, below, sibling, sibling, sibling, sibling)[i]
        lanes = pl.ds(c * CHUNK, CHUNK)
        src = images.at[:, lanes] if i < 4 else gathered.at[slot, :, lanes]
        moves[c, i] = remote(src, gathered.at[slot, :, lanes], img_send.at[7 * c + i], img_recv.at[7 * c + i], target)
        moves[c, i].start()

    def share(c):
        for arriving, passing in ((1, 5), (2, 6), (0, 4)):
            moves[c, arriving].wait_recv()
            move(c, passing)

    def complete(c):
        for i in range(3, 7):
            moves[c, i].wait_recv()

    for i in range(3):
        move(0, i)
    ctf_copies = [remote(ctf, ctfs.at[me], ctf_send.at[o - 1], ctf_recv.at[o - 1], peer(o)) for o in range(1, SLOTS)]
    for copy in ctf_copies:
        copy.start()
    for c, i in ((0, 3), (1, 0), (1, 1), (1, 2), (1, 3), (2, 0), (2, 1), (2, 2), (2, 3)):
        move(c, i)
    cross[...] = jnp.zeros_like(cross)
    squares[...] = jnp.zeros_like(squares)
    for copy in local:
        copy.wait()
    for copy in ref_copies:
        copy.wait()
    powers[...] = jnp.zeros_like(powers)

    @pl.loop(0, SHIFT)
    def _(m):
        value = powers[...]
        for j in range(4):
            v = classes[j, m].astype(F32)
            v = v * v
            value = value + (v[:, :128] + v[:, 128:])
        powers[...] = value

    for copy in ctf_copies:
        copy.wait_recv()
    noise_row = noise[...]
    for slot in range(SLOTS):
        value = ctfs[slot].astype(F32)
        factor = value * noise_row
        factors[pl.ds(slot * ROWS, ROWS), :] = twice(factor)
        curves[pl.ds(slot * ROWS, ROWS), :] = twice(factor * value)

    def prepare(c):
        @pl.loop(c * PER, (c + 1) * PER)
        def _(b):
            lanes = pl.ds(pl.multiple_of(b * WIDE, WIDE), WIDE)
            for level in range(4):
                weighted = []
                for core_slot in range(2):
                    slot = level * 2 + core_slot
                    rows = pl.ds(slot * ROWS, ROWS)
                    value = gathered[slot, :, lanes].astype(F32)
                    square = value * value
                    squares[rows, :] += square[:, :128] + square[:, 128:]
                    weighted.append(value * twice(factors[rows, :]))
                blocks[b, pl.ds(level * 2 * ROWS, 2 * ROWS), :] = jnp.concatenate(weighted, axis=0).astype(BF16)

    def score(start, stop):
        @pl.loop(start // STEP, stop // STEP)
        def _(u):
            left, right = [], []
            for v in range(STEP):
                b = u * STEP + v
                left.append(classes[lax.rem(b, 4), pl.ds(lax.div(b, 4), SHIFT)].reshape(SHIFT * HALF, WIDE))
                right.append(blocks[pl.ds(b, TURN)].reshape(TURN * PART, WIDE))
            cross[...] += dot_nt(jnp.concatenate(left, axis=1), jnp.concatenate(right, axis=1))

    share(0)
    complete(0)
    prepare(0)
    for t in range(TURN - 1):
        blocks[BLOCKS + t] = blocks[t]
    share(1)
    score(0, PER - STEP)
    complete(1)
    share(2)
    prepare(1)
    score(PER - STEP, 2 * PER - STEP)
    complete(2)
    prepare(2)
    score(2 * PER - STEP, BLOCKS)

    curve_rows = jnp.concatenate([curves[...]] * TURN, axis=0)
    square_rows = jnp.concatenate([squares[...] * twice(noise_row)] * TURN, axis=0)
    normal = dot_nt(powers[...], curve_rows, HIGHEST)
    offset = 0.5 * dot_nt(jnp.ones((8, 128), F32), square_rows, HIGHEST)
    bias = 0.5 * normal + offset[:1, :]

    def over_turns(v, op):
        v = op(v, pltpu.roll(v, 64, 1))
        return op(v, pltpu.roll(v, 128, 1))

    top = None
    for s in range(SHIFT):
        value = cross[pl.ds(s * HALF, HALF), :] - bias
        cross[pl.ds(s * HALF, HALF), :] = value
        value = jnp.max(value, axis=0, keepdims=True)
        top = value if top is None else jnp.maximum(top, value)
    top = over_turns(jnp.broadcast_to(top, (8, WIDE)), jnp.maximum)
    norm = None
    for s in range(SHIFT):
        value = jnp.exp(cross[pl.ds(s * HALF, HALF), :] - top[:1, :])
        cross[pl.ds(s * HALF, HALF), :] = value
        value = jnp.sum(value, axis=0, keepdims=True)
        norm = value if norm is None else norm + value
    norm = over_turns(jnp.broadcast_to(norm, (8, WIDE)), jnp.add)
    row = lax.broadcasted_iota(jnp.int32, (8, WIDE), 0)
    own_stats[...] = jnp.where(row < 4, top, norm)

    stat_copies = [remote(own_stats, stats.at[o - 1], st_send.at[o - 1], st_recv.at[o - 1], peer(o)) for o in range(1, SLOTS)]
    for copy in stat_copies:
        copy.start()
    for copy in stat_copies:
        copy.wait_recv()
    top, norm = top[:1, :], norm[:1, :]
    best = top
    for o in range(SLOTS - 1):
        best = jnp.maximum(best, stats[o, 0:1, :])
    mine = jnp.exp(top - best)
    norm = norm * mine
    for o in range(SLOTS - 1):
        norm = norm + stats[o, 4:5, :] * jnp.exp(stats[o, 0:1, :] - best)
    scale = mine / norm

    mass = None
    for s in range(SHIFT):
        value = (cross[pl.ds(s * HALF, HALF), :] * scale).astype(BF16)
        weights[pl.ds(s * HALF, HALF), :] = value
        value = value.astype(F32)
        mass = value if mass is None else mass + value
    denom = dot_nn(mass, curve_rows, HIGHEST)
    for k in range(4):
        bottoms[k] = denom[k * PIECE:(k + 1) * PIECE]

    def accumulate(j):
        for m in range(SHIFT):
            value = dot_nn(weights[...], blocks[pl.ds(4 * m + j, TURN)].reshape(TURN * PART, WIDE))
            for s in range(SHIFT):
                piece = value[s * HALF:(s + 1) * HALF]
                if m == 0:
                    numer[j, s] = piece
                else:
                    numer[j, (m + s) % SHIFT] += piece

    def lanes(m):
        return pl.ds(m * WIDE, WIDE)

    ends = pl.ds(QUARTER, 128), pl.ds(QUARTER + 128, 128)

    def finish_ends(ref, index, value):
        high, low = split(value)
        ref[index, :, ends[0]] = high
        ref[index, :, ends[1]] = low

    def read_ends(ref, index):
        return ref[index, :, ends[0]].astype(F32) + ref[index, :, ends[1]].astype(F32)

    def pack(j, ks):
        for k in ks:
            for m in range(SHIFT):
                parts[j, k, :, lanes(m)] = numer[j, m, pl.ds(k * PIECE, PIECE), :].astype(BF16)
            high, low = split(bottoms[k])
            parts[j, k, :, ends[0]] = high
            parts[j, k, :, ends[1]] = low

    def pass_on(j, ks, near):
        for k in ks:
            for m in range(SHIFT):
                fwd[k, :, lanes(m)] = (
                    numer[j, m, pl.ds(k * PIECE, PIECE), :] + near[k - ks[0], :, lanes(m)].astype(F32)).astype(BF16)
            finish_ends(fwd, k, bottoms[k] + read_ends(near, k - ks[0]))

    reduced = []

    def reduce_copy(src, dst, target):
        i = len(reduced)
        reduced.append(remote(src, dst, rs_send.at[i], rs_recv.at[i], target))
        reduced[i].start()
        return reduced[i]

    low, high = pl.ds(0, 2), pl.ds(2, 2)
    accumulate(opp1)
    pack(opp1, range(4))
    a = reduce_copy(parts.at[opp1, low], far_low, to_r1)
    b = reduce_copy(parts.at[opp1, high], far_high, to_l1)
    accumulate(right1)
    pack(right1, (2, 3))
    c = reduce_copy(parts.at[right1, high], plain.at[high], to_r1)
    accumulate(left1)
    pack(left1, (0, 1))
    d = reduce_copy(parts.at[left1, low], plain.at[low], to_l1)
    a.wait_recv()
    pass_on(right1, (0, 1), far_low)
    e = reduce_copy(fwd.at[low], summed.at[low], to_r1)
    b.wait_recv()
    pass_on(left1, (2, 3), far_high)
    f = reduce_copy(fwd.at[high], summed.at[high], to_l1)
    accumulate(q1)
    for copy in (c, d, e, f):
        copy.wait_recv()

    def settle(k):
        rows = pl.ds(pl.multiple_of(k * PIECE, PIECE), PIECE)
        for m in range(SHIFT):
            value = (numer[q1, m, rows, :] + plain[k, :, lanes(m)].astype(F32)) + summed[k, :, lanes(m)].astype(F32)
            total[k, :, lanes(m)] = value
            ready[k, :, lanes(m)] = value.astype(BF16)
        value = bottoms[k] + read_ends(plain, k) + read_ends(summed, k)
        total_bottom[k] = value
        finish_ends(ready, k, value)

    settle(opp2)
    far2 = reduce_copy(ready.at[opp2], two_far, to_o2)
    settle(right2)
    up2 = reduce_copy(ready.at[right2], two_left, to_r2)
    settle(left2)
    down2 = reduce_copy(ready.at[left2], two_right, to_l2)
    settle(q2)
    for copy in (up2, down2, far2):
        copy.wait_recv()
    bottom = total_bottom[q2] + twice(reg[...])
    value = total[q2]
    for ref in (two_left, two_right, two_far):
        bottom = bottom + (ref[:, ends[0]].astype(F32) + ref[:, ends[1]].astype(F32))
        value = value + ref[:, pl.ds(0, QUARTER)].astype(F32)

    def level_of(half):
        return y_hi if half == 0 else 1 - y_hi

    pieces[y_hi * 4 + q2, q1] = (value / jnp.concatenate([bottom] * (QUARTER // 128), axis=1)).astype(BF16)

    def deliver(half, v1, v2):
        index = level_of(half) * 4 + v2
        rows = pl.ds(pl.multiple_of(index * PIECE, PIECE), PIECE)
        for m in range(SHIFT):
            place = pl.ds(pl.multiple_of(v1 * WIDE + m * 4 * WIDE, WIDE), WIDE)
            out[rows, place] = pieces[index, v1, :, lanes(m)].astype(F32)

    copies = {}

    def gather(name, half, v1, v2, target):
        ref = pieces.at[level_of(half) * 4 + v2, v1]
        i = len(copies)
        copies[name] = remote(ref, ref, ag_send.at[i], ag_recv.at[i], target)
        copies[name].start()

    def arrived(*names):
        for name in names:
            copies[name].wait_recv()

    def across(half):
        gather((half, "o2"), half, q1, q2, to_o2)
        gather((half, "r2"), half, q1, q2, to_r2)
        gather((half, "l2"), half, q1, q2, to_l2)

    def spread(half, i, v2, direct=False):
        if direct:
            gather((half, "opp", i), half, q1, v2, to_o1)
        gather((half, "right", i), half, q1, v2, to_r1)
        gather((half, "left", i), half, q1, v2, to_l1)

    def relay(half, i, v2):
        if i in (0, 3):
            arrived((half, "right", i))
            gather((half, "opp", i), half, left1, v2, to_r1)
            arrived((half, "left", i))
        else:
            arrived((half, "left", i))
            gather((half, "opp", i), half, right1, v2, to_l1)
            arrived((half, "right", i))

    gather("y", 0, q1, q2, to_y)
    across(0)
    spread(0, 0, q2)
    deliver(0, q1, q2)
    arrived((0, "r2"))
    spread(0, 1, left2)
    arrived((0, "l2"))
    spread(0, 2, right2)
    arrived("y")
    across(1)
    spread(1, 0, q2)
    relay(0, 0, q2)
    arrived((0, "o2"))
    spread(0, 3, opp2)
    for v1, v2 in ((q1, left2), (q1, right2), (q1, opp2), (left1, q2), (right1, q2)):
        deliver(0, v1, v2)
    deliver(1, q1, q2)
    relay(0, 1, left2)
    relay(0, 2, right2)
    arrived((1, "r2"))
    spread(1, 1, left2, True)
    arrived((1, "l2"))
    spread(1, 2, right2, True)
    relay(1, 0, q2)
    arrived((1, "o2"))
    spread(1, 3, opp2, True)
    relay(0, 3, opp2)
    for v1 in (left1, right1):
        for v2 in (left2, right2, opp2):
            deliver(0, v1, v2)
    for v2 in (left2, right2, opp2):
        deliver(1, q1, v2)
    for v1 in (left1, right1):
        deliver(1, v1, q2)
    for i, v2 in ((0, q2), (1, left2), (2, right2), (3, opp2)):
        arrived((0, "opp", i))
        deliver(0, opp1, v2)
    arrived((1, "opp", 0))
    deliver(1, opp1, q2)
    for i, v2 in ((1, left2), (2, right2), (3, opp2)):
        arrived((1, "right", i), (1, "left", i))
        deliver(1, left1, v2)
        deliver(1, right1, v2)
    for i, v2 in ((1, left2), (2, right2), (3, opp2)):
        arrived((1, "opp", i))
        deliver(1, opp1, v2)
    for copy in list(moves.values()) + ctf_copies + stat_copies + reduced + list(copies.values()):
        copy.wait_send()


def body(images, ctf, refs, noise_inv, reg):
    hbm = pl.BlockSpec(memory_space=pltpu.MemorySpace.HBM)
    dma = pltpu.SemaphoreType.DMA
    vmem = pltpu.VMEM
    near = vmem((2, PIECE, FULL), BF16)
    four = vmem((4, PIECE, FULL), BF16)
    two = vmem((PIECE, FULL), BF16)
    return pl.pallas_call(
        kernel,
        out_shape=jax.ShapeDtypeStruct((2 * HALF, PIX), F32),
        in_specs=[hbm] * 5,
        out_specs=pl.BlockSpec(memory_space=pltpu.VMEM),
        scratch_shapes=[
            vmem((SLOTS, ROWS, PIX), BF16),
            vmem((SLOTS, ROWS, CYCLES), BF16),
            vmem((BLOCKS + TURN - 1, PART, WIDE), BF16),
            vmem((4, 2 * SHIFT - 1, HALF, WIDE), BF16),
            vmem((1, CYCLES), F32),
            vmem((1, CYCLES), F32),
            vmem((PART, 128), F32),
            vmem((PART, 128), F32),
            vmem((PART, 128), F32),
            vmem((HALF, 128), F32),
            vmem((SHIFT * HALF, TURN * PART), F32),
            vmem((SHIFT * HALF, TURN * PART), BF16),
            vmem((SLOTS - 1, 8, WIDE), F32),
            vmem((8, WIDE), F32),
            vmem((4, SHIFT, HALF, WIDE), F32),
            vmem((4, PIECE, 128), F32),
            vmem((4, 4, PIECE, FULL), BF16),
            near, near, four, four, four,
            vmem((4, PIECE, QUARTER), F32),
            vmem((4, PIECE, 128), F32),
            four,
            two, two, two,
            vmem((8, 4, PIECE, QUARTER), BF16),
            dma((7 * CHUNKS,)), dma((7 * CHUNKS,)), dma((7,)), dma((7,)), dma((7,)), dma((7,)), dma((4,)),
            dma((4 * (2 * SHIFT - 1),)), dma((9,)), dma((9,)), dma((31,)), dma((31,)),
        ],
        compiler_params=pltpu.CompilerParams(
            collective_id=0, has_side_effects=True, vmem_limit_bytes=40 * 1024 * 1024),
        name="step",
    )(*[pltpu.with_memory_space_constraint(v, pltpu.MemorySpace.HBM) for v in (images, ctf, refs, noise_inv.reshape(1, CYCLES), reg.reshape(1, CYCLES))])


def solution(mesh):
    in_specs = (P(("cls", "grp"), None), P(("cls", "grp"), None), P("cls", None), P(), P())
    return jax.shard_map(body, mesh=mesh, in_specs=in_specs, out_specs=P("cls", None), check_vma=False)
```
